32 devices in a mesh: section: 4 (over y, x), tm: 8 (over z, core).
Axes of the slice: x: 2, y: 2, z: 4, core: 2. Of those that a mesh axis runs over, the one named last changes fastest.
Arguments:
- inputs: bfloat16 [3, 1024, 1024], P(None, 'tm', 'section'), may hold values from -6 to 6
- lengths: int32 [3], replicated, may hold values from 256 to 1024, as said below
- w_expand: bfloat16 [2, 4, 1024, 2048], P(None, 'section'), may hold values from -0.1875 to 0.1875
- w_project: bfloat16 [2, 4, 1024, 1024], P(None, 'section'), may hold values from -0.1875 to 0.1875
- kernel: float32 [2, 4, 32, 1024], P(None, 'section'), may hold values from -1.5 to 1.5
- gain: float32 [2, 4, 1024], P(None, 'section'), may hold values from 0.1 to 1.9
Outputs:
- encoded: bfloat16 [3, 1024, 1024], P(None, 'tm', 'section')
The draws below stay inside these ranges and needn't reach their ends.
Inputs may be any that keep to these rules, and one draw needn't show every extreme that they name: lengths[0] is 1024.
All inputs are finite; a program needn't handle non-finite values.
Results may differ from the reference program's by a relative error of at most 0.022.
Values may be sent and summed in bfloat16 or wider, within the bound.
No kernel may reach another device: no remote copies, remote signals or barrier semaphores. Data moves between devices by JAX's collectives and lax.ppermute only.
A program may use at most 64 MiB of HBM per device.

```python
import jax
import jax.numpy as jnp
from jax import lax

D = 1024
KW = 32
PASSES = 2
MB = 3
FRAMES = 1024
N_SECTION = 4


def draw_lengths(key, part):
    values = jax.random.randint(key, (MB,), FRAMES // 4, FRAMES + 1)
    return jnp.where(jnp.arange(MB) == 0, FRAMES, values).astype(jnp.int32)


def shard_levels(own_key, dims, cuts, least, high):
    level = 1.0
    for dim, blocks in cuts:
        heights = jax.random.uniform(jax.random.fold_in(jax.random.fold_in(own_key, 6), dim), (blocks,), jnp.float32, least / len(cuts), high / len(cuts))
        level = level * jnp.repeat(jnp.exp(heights), dims[dim] // blocks).reshape((-1,) + (1,) * (len(dims) - 1 - dim))
    return level


def scatter_about(own_key, extent, spread, reach, pieces=(), held_as=jnp.bfloat16):
    array = spread * jax.random.normal(own_key, extent, jnp.float32)
    if pieces:
        array = array * shard_levels(own_key, extent, pieces, -0.22, 0.18)
    return jnp.clip(array, -reach, reach).astype(held_as)


def setup_inputs(seed: int = 0) -> dict:
    splits = jax.random.split(jax.random.key(seed), 7)
    return {
        "inputs": scatter_about(splits[0], (MB, FRAMES, D), 1.0, 6.0, ((1, 8), (2, 4))),
        "lengths": draw_lengths(jax.random.fold_in(splits[6], 71), 0),
        "w_expand": scatter_about(splits[2], (PASSES, N_SECTION, D, 2 * D), D ** -0.5, 0.1875, ((1, 4),)),
        "w_project": scatter_about(splits[3], (PASSES, N_SECTION, D, D), D ** -0.5, 0.1875, ((1, 4),)),
        "kernel": scatter_about(splits[4], (PASSES, N_SECTION, KW, D), (KW // 2) ** -0.5, 1.5, ((1, 4),), jnp.float32),
        "gain": jnp.clip(1.0 + 0.18 * jax.random.normal(splits[5], (PASSES, N_SECTION, D), jnp.float32), 0.1, 1.9),
    }


def layer_norm(values):
    center = values - lax.optimization_barrier(jnp.mean(values, axis=-1, keepdims=True))
    variance = lax.optimization_barrier(jnp.mean(center * center, axis=-1, keepdims=True))
    return center * lax.rsqrt(variance + 1e-05)

def conv_layer(stream, frame_mask, w_first, w_second, taps, scale):
    feats = stream.shape[1]
    normed = (layer_norm(stream.astype(jnp.float32)) * scale).astype(jnp.bfloat16)
    expanded = jnp.dot(normed, w_first, preferred_element_type=jnp.float32)
    gated = (expanded[:, :feats] * jax.nn.sigmoid(expanded[:, feats:]) * frame_mask[:, None]).astype(jnp.bfloat16)
    width = taps.shape[0]
    padded = jnp.concatenate([jnp.zeros((width - 1, feats), jnp.bfloat16), gated], axis=0)
    count = stream.shape[0]
    depthwise = jnp.zeros((count, feats), jnp.float32)
    for offset in range(width):
        depthwise = depthwise + taps[offset][None, :] * padded[offset:offset + count].astype(jnp.float32)
    activated = jax.nn.silu(layer_norm(depthwise)).astype(jnp.bfloat16)
    summed = stream.astype(jnp.float32) + jnp.dot(activated, w_second, preferred_element_type=jnp.float32)
    return (summed * frame_mask[:, None]).astype(jnp.bfloat16)

def reference(inputs, lengths, w_expand, w_project, kernel, gain):
    positions = jnp.arange(FRAMES, dtype=jnp.int32)
    results = []
    for micro in range(MB):
        frame_mask = (positions < lengths[micro]).astype(jnp.float32)
        stream = inputs[micro]
        for pass_idx in range(PASSES):
            for section_idx in range(N_SECTION):
                stream = conv_layer(stream, frame_mask, w_expand[pass_idx, section_idx], w_project[pass_idx, section_idx], kernel[pass_idx, section_idx], gain[pass_idx, section_idx])
        results.append(stream)
    return jnp.stack(results, axis=0)
```

```python
import functools

import jax
import jax.numpy as jnp
from jax import lax
from jax.experimental import pallas as pl
from jax.experimental.pallas import tpu as pltpu
from jax.sharding import PartitionSpec as P

SPAN = 256
LANES = 128
SUB = 8


def rotated(value, axis, steps):
    count = lax.axis_size(axis)
    pairs = [(source, (source + steps) % count) for source in range(count)]
    return lax.ppermute(value, axis, pairs)


def rotated_both(value, steps, frame_steps):
    sections = lax.axis_size("section")
    blocks = lax.axis_size("tm")
    pairs = []
    for section in range(sections):
        for block in range(blocks):
            target = ((section + steps) % sections) * blocks + (block + frame_steps) % blocks
            pairs.append((section * blocks + block, target))
    return lax.ppermute(value, ("section", "tm"), pairs)


def normalized(values):
    center = values - jnp.mean(values, axis=-1, keepdims=True)
    variance = jnp.mean(center * center, axis=-1, keepdims=True)
    return center * lax.rsqrt(variance + 1e-05)


def conv_columns(gated, taps, rows, halo):
    width = taps.shape[0]
    lead = halo - width + 1
    total = None
    for shift in range(SUB):
        partial = None
        for tap in range(width):
            if (tap + lead) % SUB != shift:
                continue
            start = tap + lead - shift
            count = rows if shift == 0 else rows + SUB
            term = taps[tap : tap + 1] * gated[start : start + count]
            partial = term if partial is None else partial + term
        if partial is None:
            continue
        if shift:
            partial = pltpu.roll(partial, rows + SUB - shift, 0)[:rows]
        total = partial if total is None else total + partial
    return total


def layer_kernel(
    slot, scalars, x_ref, rim_ref, w_first, w_second, taps_ref, scale_ref, y_ref, tail_ref, normed, depthwise
):
    rows, feats = x_ref.shape
    halo = rim_ref.shape[0]

    @pl.when(scalars[slot, 0] > 0)
    def _():
        which = scalars[slot, 1]
        first_row = scalars[slot, 2]
        last_row = scalars[slot, 3]
        scale = scale_ref[pl.ds(which, 1), :]
        stream = x_ref[...].astype(jnp.float32)
        normed[:halo, :] = (normalized(rim_ref[...].astype(jnp.float32)) * scale).astype(jnp.bfloat16)
        normed[halo:, :] = (normalized(stream) * scale).astype(jnp.bfloat16)
        position = lax.broadcasted_iota(jnp.int32, (halo + rows, 1), 0) - halo
        kept = (position >= first_row) & (position < last_row)
        for begin in range(0, feats, SPAN):
            value = jnp.dot(
                normed[...], w_first[which, :, begin : begin + SPAN], preferred_element_type=jnp.float32
            )
            gate = jnp.dot(
                normed[...],
                w_first[which, :, feats + begin : feats + begin + SPAN],
                preferred_element_type=jnp.float32,
            )
            gated = jnp.where(kept, value * jax.nn.sigmoid(gate), 0.0)
            gated = gated.astype(jnp.bfloat16).astype(jnp.float32)
            for lane in range(0, SPAN, LANES):
                depthwise[:, begin + lane : begin + lane + LANES] = conv_columns(
                    gated[:, lane : lane + LANES],
                    taps_ref[which, :, begin + lane : begin + lane + LANES],
                    rows,
                    halo,
                )
        activated = jax.nn.silu(normalized(depthwise[...])).astype(jnp.bfloat16)
        row_kept = kept[halo:]
        for begin in range(0, feats, SPAN):
            added = jnp.dot(
                activated, w_second[which, :, begin : begin + SPAN], preferred_element_type=jnp.float32
            )
            summed = x_ref[:, begin : begin + SPAN].astype(jnp.float32) + added
            result = jnp.where(row_kept, summed, 0.0).astype(jnp.bfloat16)
            y_ref[:, begin : begin + SPAN] = result
            tail_ref[:, begin : begin + SPAN] = result[rows - halo :]


def conv_layer(slot, scalars, x, rim, w_first, w_second, taps, scale):
    rows, feats = x.shape
    halo = rim.shape[0]
    vmem = pl.BlockSpec(memory_space=pltpu.VMEM)
    return pl.pallas_call(
        functools.partial(layer_kernel, slot),
        out_shape=(
            jax.ShapeDtypeStruct((rows, feats), jnp.bfloat16),
            jax.ShapeDtypeStruct((halo, feats), jnp.bfloat16),
        ),
        in_specs=[pl.BlockSpec(memory_space=pltpu.SMEM)] + [vmem] * 6,
        out_specs=(vmem, vmem),
        scratch_shapes=[
            pltpu.VMEM((halo + rows, feats), jnp.bfloat16),
            pltpu.VMEM((rows, feats), jnp.float32),
        ],
        name="conv_layer",
    )(scalars, x, rim, w_first, w_second, taps, scale)


def per_device(inputs, lengths, w_expand, w_project, kernel, gain):
    sections = lax.axis_size("section")
    section_idx = lax.axis_index("section")
    block_idx = lax.axis_index("tm")
    micro, rows, _ = inputs.shape
    passes = w_expand.shape[0]
    feats = w_expand.shape[2]
    width = kernel.shape[2]
    halo = -(-(width - 1) // 16) * 16
    lag = max(2, -(-micro // sections))
    period = lag * sections
    layers = passes * sections
    slots = micro + lag * (layers - 1)

    lane = jnp.arange(slots, dtype=jnp.int32) - lag * section_idx
    pass_of = jnp.clip(lane // period, 0, passes - 1)
    micro_of = lane - pass_of * period
    active = (lane >= 0) & (micro_of < micro)
    micro_of = jnp.clip(micro_of, 0, micro - 1)
    origin = block_idx * rows
    length_of = jnp.zeros((slots,), jnp.int32)
    for m in range(micro):
        length_of = jnp.where(micro_of == m, lengths[m], length_of)
    scalars = jnp.stack(
        [active.astype(jnp.int32), pass_of, jnp.full((slots,), -origin, jnp.int32), length_of - origin], axis=1
    )

    w_first, w_second, taps, scale = w_expand[:, 0], w_project[:, 0], kernel[:, 0], gain[:, 0]

    edge = rotated(inputs[:, rows - halo :], "tm", 1)
    blocks = jnp.concatenate([edge, inputs], axis=1)
    fresh = []
    for m in range(micro):
        pieces = [blocks[m]] + [rotated(blocks[m], "section", -step) for step in range(1, sections)]
        fresh.append(jnp.concatenate(pieces, axis=1))

    results = [None] * slots
    arrived = [None] * slots
    finished = []
    for slot in range(slots):
        source = arrived[slot - lag] if slot >= lag else None
        if slot < micro:
            x, rim = fresh[slot][halo:], fresh[slot][:halo]
            if source is not None:
                x = jnp.where(section_idx == 0, x, source[0])
                rim = jnp.where(section_idx == 0, rim, source[1])
        else:
            x, rim = source
        y, tail = conv_layer(slot, scalars, x, rim, w_first, w_second, taps, scale)
        if slot < slots - lag:
            arrived[slot] = (rotated(y, "section", 1), rotated_both(tail, 1, 1))
        if slot >= slots - micro:
            finished.append(y)

    part = feats // sections
    outs = []
    for y in finished:
        out = None
        for step in range(sections):
            target = (section_idx + step) % sections
            piece = lax.dynamic_slice_in_dim(y, target * part, part, axis=1)
            if step:
                piece = rotated(piece, "section", step)
            out = piece if out is None else jnp.where(section_idx == (sections - 1 + step) % sections, piece, out)
        outs.append(out)
    return jnp.stack(outs, axis=0)


def solution(mesh):
    in_specs = (
        P(None, "tm", "section"),
        P(),
        P(None, "section", None, None),
        P(None, "section", None, None),
        P(None, "section", None, None),
        P(None, "section", None),
    )
    out_specs = P(None, "tm", "section")
    return jax.shard_map(
        per_device, mesh=mesh, in_specs=in_specs, out_specs=out_specs, check_vma=False
    )
```

```python
import functools

import jax
import jax.numpy as jnp
from jax import lax
from jax.experimental import pallas as pl
from jax.experimental.pallas import tpu as pltpu
from jax.sharding import PartitionSpec as P

SPAN = 256
LANES = 128
SUB = 8
BAND = 32
VMEM_LIMIT = 16 * 1024 * 1024
VMEM = pl.BlockSpec(memory_space=pltpu.VMEM)
TOKEN = jax.ShapeDtypeStruct((SUB, LANES), jnp.float32)


def rotated(value, axis, steps):
    count = lax.axis_size(axis)
    pairs = [(source, (source + steps) % count) for source in range(count)]
    return lax.ppermute(value, axis, pairs)


def rotated_both(value, steps, frame_steps):
    sections = lax.axis_size("section")
    blocks = lax.axis_size("tm")
    pairs = []
    for section in range(sections):
        for block in range(blocks):
            target = ((section + steps) % sections) * blocks + (block + frame_steps) % blocks
            pairs.append((section * blocks + block, target))
    return lax.ppermute(value, ("section", "tm"), pairs)


def normalized(values):
    center = values - jnp.mean(values, axis=-1, keepdims=True)
    variance = jnp.mean(center * center, axis=-1, keepdims=True)
    return center * lax.rsqrt(variance + 1e-05)


def conv_columns(gated, taps, rows, halo):
    width = taps.shape[0]
    lead = halo - width + 1
    total = None
    for shift in range(SUB):
        partial = None
        for tap in range(width):
            if (tap + lead) % SUB != shift:
                continue
            start = tap + lead - shift
            count = rows if shift == 0 else rows + SUB
            term = taps[tap : tap + 1] * gated[start : start + count]
            partial = term if partial is None else partial + term
        if partial is None:
            continue
        if shift:
            partial = pltpu.roll(partial, rows + SUB - shift, 0)[:rows]
        total = partial if total is None else total + partial
    return total


def span_at(index):
    return pl.ds(pl.multiple_of(index * SPAN, SPAN), SPAN)


def layer_body(first_row, last_row, held, w_first, w_second, taps_ref, scale_ref, store, scratch):
    normed, gated_ref, depthwise, activated = scratch
    height, feats = held.shape
    rows = depthwise.shape[0]
    halo = height - rows
    spans = feats // SPAN
    scale = scale_ref[...]

    def norm_band(band, carry):
        at = pl.ds(pl.multiple_of(band * BAND, BAND), BAND)
        normed[at, :] = (normalized(held[at, :].astype(jnp.float32)) * scale).astype(jnp.bfloat16)
        return carry

    lax.fori_loop(0, height // BAND, norm_band, 0)
    position = lax.broadcasted_iota(jnp.int32, (height, 1), 0) - halo
    kept = (position >= first_row) & (position < last_row)

    def gate_span(span):
        value = jnp.dot(normed[...], w_first[:, span_at(span)], preferred_element_type=jnp.float32)
        gate = jnp.dot(normed[...], w_first[:, span_at(spans + span)], preferred_element_type=jnp.float32)
        gated = jnp.where(kept, value * jax.nn.sigmoid(gate), 0.0)
        gated_ref[span % 2] = gated.astype(jnp.bfloat16).astype(jnp.float32)

    def conv_span(span):
        for lane in range(0, SPAN, LANES):
            at = pl.ds(pl.multiple_of(span * SPAN + lane, LANES), LANES)
            depthwise[:, at] = conv_columns(
                gated_ref[span % 2, :, lane : lane + LANES], taps_ref[:, at], rows, halo
            )

    def both(span, carry):
        conv_span(span - 1)
        gate_span(span)
        return carry

    gate_span(0)
    lax.fori_loop(1, spans, both, 0)
    conv_span(spans - 1)

    def act_band(band, carry):
        at = pl.ds(pl.multiple_of(band * BAND, BAND), BAND)
        activated[at, :] = jax.nn.silu(normalized(depthwise[at, :])).astype(jnp.bfloat16)
        return carry

    lax.fori_loop(0, rows // BAND, act_band, 0)

    def project_span(span, carry):
        added = jnp.dot(activated[...], w_second[:, span_at(span)], preferred_element_type=jnp.float32)
        summed = held[halo:, span_at(span)].astype(jnp.float32) + added
        store(span, jnp.where(kept[halo:], summed, 0.0).astype(jnp.bfloat16))
        return carry

    lax.fori_loop(0, spans, project_span, 0)


def layer_kernel(slot, lag, sections, chosen, behind, fresh, last, lengths, _, *refs):
    carried = refs[:behind]
    pieces = refs[len(carried) : len(carried) + fresh]
    weights = refs[len(carried) + fresh : len(carried) + fresh + 4 * len(chosen)]
    outs = refs[len(carried) + fresh + 4 * len(chosen) :]
    outs, held, scratch = outs[:-5], outs[-5], outs[-4:]
    token = outs[-1]
    rows = scratch[2].shape[0]
    halo = held.shape[0] - rows
    micro = lengths.shape[0]
    section = lax.axis_index("section")
    token[...] = jnp.zeros_like(token)
    first_row = -rows * lax.axis_index("tm")

    def store(span, result):
        outs[0][:, span_at(span)] = result
        if not last:
            outs[1][:, span_at(span)] = result[rows - halo :]

    for order, which in enumerate(chosen):
        item = slot - lag * (section + sections * which)

        @pl.when((item >= 0) & (item < micro))
        def _():
            if carried:
                held[:halo, :] = carried[1][...]
                held[halo:, :] = carried[0][...]
            if fresh:

                @pl.when(section == 0)
                def _():
                    for index, piece in enumerate(pieces):
                        part = piece.shape[-1]
                        held[:, index * part : (index + 1) * part] = piece[...]

            last_row = lengths[pl.ds(jnp.clip(item, 0, micro - 1), 1), :][:, :1] + first_row
            layer_body(first_row, last_row, held, *weights[4 * order : 4 * order + 4], store, scratch)


def conv_layer(slot, lag, sections, chosen, lengths, token, carried, pieces, weights, shape, last):
    rows, halo, feats = shape
    fresh = len(pieces)
    out_shape = [jax.ShapeDtypeStruct((rows, feats), jnp.bfloat16)]
    if not last:
        out_shape.append(jax.ShapeDtypeStruct((halo, feats), jnp.bfloat16))
    operands = [*carried, *pieces, *weights]
    return pl.pallas_call(
        functools.partial(layer_kernel, slot, lag, sections, chosen, len(carried), fresh, last),
        out_shape=(*out_shape, TOKEN),
        in_specs=[VMEM] * (2 + len(operands)),
        out_specs=(*[VMEM for _ in out_shape], VMEM),
        scratch_shapes=[
            pltpu.VMEM((halo + rows, feats), jnp.bfloat16),
            pltpu.VMEM((halo + rows, feats), jnp.bfloat16),
            pltpu.VMEM((2, halo + rows, SPAN), jnp.float32),
            pltpu.VMEM((rows, feats), jnp.float32),
            pltpu.VMEM((rows, feats), jnp.bfloat16),
        ],
        compiler_params=pltpu.CompilerParams(vmem_limit_bytes=VMEM_LIMIT),
        name="conv_layer",
    )(lengths, token, *operands)


def fetch_kernel(which, _, *refs):
    count = (len(refs) - 2) // 2
    copies = [
        pltpu.make_async_copy(refs[i].at[which, 0], refs[count + i], refs[-1].at[i]) for i in range(count)
    ]
    for copy in copies:
        copy.start()
    refs[-2][...] = jnp.zeros_like(refs[-2])
    for copy in copies:
        copy.wait()


def fetched(which, token, *arrays):
    count = len(arrays)
    *found, token = pl.pallas_call(
        functools.partial(fetch_kernel, which),
        out_shape=tuple(jax.ShapeDtypeStruct(array.shape[2:], array.dtype) for array in arrays) + (TOKEN,),
        in_specs=[VMEM] + [pl.BlockSpec(memory_space=pltpu.HBM)] * count,
        out_specs=tuple(VMEM for _ in arrays) + (VMEM,),
        scratch_shapes=[pltpu.SemaphoreType.DMA((count,))],
        compiler_params=pltpu.CompilerParams(vmem_limit_bytes=VMEM_LIMIT),
        cost_estimate=pl.CostEstimate(flops=0, transcendentals=0, bytes_accessed=0),
        name="fetch",
    )(token, *arrays)
    return found, token


def pack_kernel(edge, inputs, *outs):
    halo = edge.shape[1]
    for index, out in enumerate(outs):
        out[:halo, :] = edge[index]
        out[halo:, :] = inputs[index]


def packed(edge, inputs):
    micro, rows, part = inputs.shape
    halo = edge.shape[1]
    return pl.pallas_call(
        pack_kernel,
        out_shape=tuple(jax.ShapeDtypeStruct((halo + rows, part), inputs.dtype) for _ in range(micro)),
        in_specs=[VMEM, VMEM],
        out_specs=tuple(VMEM for _ in range(micro)),
        compiler_params=pltpu.CompilerParams(vmem_limit_bytes=VMEM_LIMIT),
        name="pack",
    )(edge, inputs)


def split_kernel(y, *pieces):
    sections = len(pieces)
    part = pieces[0].shape[1]
    section = lax.axis_index("section")
    for step, piece in enumerate(pieces):
        target = lax.rem(section + step, sections)
        piece[...] = y[:, pl.ds(pl.multiple_of(target * part, part), part)]


def split(y, sections):
    rows, feats = y.shape
    part = feats // sections
    return pl.pallas_call(
        split_kernel,
        out_shape=tuple(jax.ShapeDtypeStruct((rows, part), y.dtype) for _ in range(sections)),
        in_specs=[VMEM],
        out_specs=tuple(VMEM for _ in range(sections)),
        compiler_params=pltpu.CompilerParams(vmem_limit_bytes=VMEM_LIMIT),
        name="split",
    )(y)


def join_kernel(sections, *refs):
    pieces, out = refs[:-1], refs[-1]
    section = lax.axis_index("section")
    for step in range(sections):

        @pl.when(section == (sections - 1 + step) % sections)
        def _():
            for index in range(out.shape[0]):
                out[index] = pieces[index * sections + step][...]


def joined(pieces, sections):
    rows, part = pieces[0].shape
    return pl.pallas_call(
        functools.partial(join_kernel, sections),
        out_shape=jax.ShapeDtypeStruct((len(pieces) // sections, rows, part), pieces[0].dtype),
        in_specs=[VMEM] * len(pieces),
        out_specs=VMEM,
        compiler_params=pltpu.CompilerParams(vmem_limit_bytes=VMEM_LIMIT),
        name="join",
    )(*pieces)


def per_device(inputs, lengths, w_expand, w_project, kernel, gain):
    sections = lax.axis_size("section")
    micro, rows, _ = inputs.shape
    passes = w_expand.shape[0]
    feats = w_expand.shape[2]
    width = kernel.shape[2]
    halo = -(-(width - 1) // BAND) * BAND
    lag = max(2, -(-micro // sections))
    period = lag * sections
    slots = micro + lag * (passes * sections - 1)
    shape = (rows, halo, feats)

    token = jnp.zeros(TOKEN.shape, TOKEN.dtype)
    limits = jnp.broadcast_to(lengths[:, None], (micro, LANES))
    gain = gain[:, :, None]
    layer_weights = []
    edge = rotated(inputs[:, rows - halo :], "tm", 1)
    blocks = packed(edge, inputs)
    pieces = [
        [blocks[m]] + [rotated(blocks[m], "section", -step) for step in range(1, sections)] for m in range(micro)
    ]

    arrived = [None] * slots
    finished = []
    for slot in range(slots):
        wanted = min((slot + 3) // period, passes - 1)
        while len(layer_weights) <= wanted:
            weights, token = fetched(len(layer_weights), token, w_expand, w_project, kernel, gain)
            layer_weights.append(weights)
        carried = arrived[slot - lag] if slot >= lag else ()
        fresh = pieces[slot] if slot < micro else ()
        chosen = [p for p in range(passes) if 0 <= slot - p * period < lag * (sections - 1) + micro]
        weights = [array for p in chosen for array in layer_weights[p]]
        last = slot >= slots - lag
        *result, token = conv_layer(slot, lag, sections, chosen, limits, token, carried, fresh, weights, shape, last)
        if not last:
            rim = rotated_both(result[1], 1, 1)
            arrived[slot] = (rotated(result[0], "section", 1), rim)
        if slot >= slots - micro:
            own, *others = split(result[0], sections)
            finished += [own] + [rotated(piece, "section", step + 1) for step, piece in enumerate(others)]
    return joined(finished, sections)


def solution(mesh):
    in_specs = (
        P(None, "tm", "section"),
        P(),
        P(None, "section", None, None),
        P(None, "section", None, None),
        P(None, "section", None, None),
        P(None, "section", None),
    )
    out_specs = P(None, "tm", "section")
    return jax.shard_map(
        per_device, mesh=mesh, in_specs=in_specs, out_specs=out_specs, check_vma=False
    )
```
